32 devices in a mesh: row: 8 (over y, x, core), col: 4 (over z).
Axes of the slice: x: 2, y: 2, z: 4, core: 2. Of those that a mesh axis runs over, the one named last changes fastest.
Arguments:
- a_blocks: bfloat16 [1024, 16, 128, 128], P(('row', 'col')), may hold values from -0.0625 to 0.0625
- omega: bfloat16 [16384, 256], P('col'), may hold values from -6 to 6
- route_dest: int32 [1024, 1], P(('row', 'col')), may hold values from 0 to 7; in each aligned block of 32 rows (0 to 31, 32 to 63, ...) at most 4 rows name the same one
- row_target: int32 [1024], P(('row', 'col')), may hold values from 0 to 31
- col_target: int32 [1024, 16], P(('row', 'col')), may hold values from 0 to 31
Outputs:
- basis: float32 [32768, 256], P(('row', 'col'))
- factor: float32 [256, 256], replicated
The draws below stay inside these ranges and needn't reach their ends.
Inputs may be any that keep to these rules, and one draw needn't show every extreme that they name: `route_dest`: among the 32 rows of one device no value appears more than 4 times, and in some device's rows one value appears exactly 4 times.
All inputs are finite; a program needn't handle non-finite values.
Results may differ from the reference program's by a relative error of at most 0.003.
Values may be sent and summed in bfloat16 or wider, within the bound.
A program may use at most 192 MiB of HBM per device.

```python
import math
import jax
import jax.numpy as jnp
import numpy as np
from jax import lax

BS = 128
SKETCH = 256
RB_DEV = 8
NT = 32
GRP = 16
CB_DEV = 32
CAP = 4
TARGETS = 1024
OMEGA_ROWS = 16384
N_ROW = 8
N_COL = 4


def place_ends(result, own_key, least, top_value):
    extent = result.shape
    index_at = [jax.random.randint(jax.random.fold_in(own_key, axis), (), 0, extent[axis]) for axis in range(len(extent))]
    result = result.at[tuple(index_at)].set(least)
    longest = extent.index(max(extent))
    index_at[longest] = (index_at[longest] + 1) % extent[longest]
    return result.at[tuple(index_at)].set(top_value)


def block_levels(key, extent, cuts, smallest, high):
    level = 1.0
    for dim, blocks in cuts:
        heights = jax.random.uniform(jax.random.fold_in(jax.random.fold_in(key, 6), dim), (blocks,), jnp.float32, smallest / len(cuts), high / len(cuts))
        level = level * jnp.repeat(jnp.exp(heights), extent[dim] // blocks).reshape((-1,) + (1,) * (len(extent) - 1 - dim))
    return level


def assign_block(stream_key, own, number, rows, count, top, limit, skew):
    ranking = jax.random.permutation(stream_key, count)
    crowded, usual = load_shares(count, rows * top, limit, skew, True), load_shares(count, rows * top, limit, skew, False)
    places = jnp.arange(count)

    def named(sizes, rotation):
        used = int((sizes > 0).sum())
        fixed = max(1, used // 4)
        passed = fixed + (places - fixed + rotation * (used - fixed)) % max(1, count - fixed)
        return jnp.zeros((count,), jnp.int32).at[ranking[jnp.where(places < fixed, places, passed)]].set(jnp.asarray(sizes, jnp.int32))

    sizes = jnp.where(number % 4 == 0, named(crowded, number // 4), named(usual, number - number // 4 - 1))
    mixed = jax.random.permutation(jax.random.fold_in(own, 3), count)
    donor, receiver = mixed[0:count // 2 * 2:2], mixed[1:count // 2 * 2:2]
    margin = jnp.minimum(sizes[donor] - 1, limit - sizes[receiver]) // 2
    margin = jnp.where((donor == ranking[0]) | (receiver == ranking[0]) | (sizes[receiver] == 0), 0, jnp.maximum(margin, 0))
    passed = jax.random.randint(jax.random.fold_in(own, 4), (count // 2,), 0, 1 << 20) % (margin + 1)
    sizes = sizes.at[donor].add(-passed).at[receiver].add(passed)
    items = jnp.searchsorted(jnp.cumsum(sizes), jnp.arange(rows * top), side="right").astype(jnp.int32)
    grid = items.reshape(top, rows).T
    grid = grid[jax.random.permutation(jax.random.fold_in(own, 1), rows)]
    rotation = jax.random.randint(jax.random.fold_in(own, 2), (rows, 1), 0, top)
    return jnp.take_along_axis(grid, (jnp.arange(top)[None, :] + rotation) % top, axis=1)


def load_shares(number_of, total, most, slope, full):
    loads = [(1 << 20) // math.isqrt(rank ** slope) + 1 for rank in range(1, number_of + 1)]
    largest = most if full else min(most, max(-(-total // number_of), total * loads[0] // sum(loads)))
    least = 1 if total - largest >= number_of - 1 else 0
    given, surplus = [largest] + [least] * (number_of - 1), total - largest - least * (number_of - 1)
    while surplus > 0:
        movable = [i for i in range(1, number_of) if given[i] < largest] or [i for i in range(1, number_of) if given[i] < most]
        mass, remaining = sum([loads[i] for i in movable]), surplus
        for i in movable:
            extra = min(most - given[i], max(1, remaining * loads[i] // mass), surplus)
            given[i] = given[i] + extra
            surplus = surplus - extra
    return np.array(given)


def bell_draw(own_key, extent, width, limit, pieces=(), held_as=jnp.bfloat16):
    gain = block_levels(own_key, extent, pieces, -0.22, 0.18) if pieces else 1.0
    result = jax.random.normal(own_key, extent, jnp.float32) * width * gain
    return jnp.minimum(jnp.maximum(result, -limit), limit).astype(held_as)


def setup_inputs(seed: int = 0) -> dict:
    seeds = jax.random.split(jax.random.key(seed), 6)
    a_blocks = bell_draw(seeds[0], (TARGETS, GRP, BS, BS), (BS * GRP * NT // RB_DEV) ** -0.5, 0.0625, ((0, 32),))
    omega = bell_draw(seeds[1], (OMEGA_ROWS, SKETCH), 1.0, 6.0, ((0, 4),))
    route_dest_keys = jax.random.split(jax.random.fold_in(seeds[2], 1), TARGETS // NT)
    route_dest_turns = jax.random.permutation(jax.random.fold_in(seeds[2], 3), TARGETS // NT)
    route_dest = jax.vmap(lambda own, number: assign_block(jax.random.fold_in(seeds[2], 2), own, number, NT, N_ROW, 1, CAP, 1))(route_dest_keys, route_dest_turns).reshape((TARGETS, 1))
    row_target = place_ends(jax.random.randint(seeds[3], (TARGETS,), 0, RB_DEV * N_COL), jax.random.fold_in(seeds[3], 1), 0, (RB_DEV * N_COL) - 1).astype(jnp.int32)
    col_target = place_ends(jax.random.randint(seeds[4], (TARGETS, GRP), 0, CB_DEV), jax.random.fold_in(seeds[4], 1), 0, CB_DEV - 1).astype(jnp.int32)
    return dict(a_blocks=a_blocks, omega=omega, route_dest=route_dest, row_target=row_target, col_target=col_target)


def reference(a_blocks, omega, route_dest, row_target, col_target):
    devices = N_ROW * N_COL
    group_blocks = RB_DEV * N_COL
    slabs = omega.reshape(N_COL, CB_DEV, BS, SKETCH)
    blocks = a_blocks.reshape(devices, NT, GRP, BS, BS)
    targets = (route_dest[:, 0] * group_blocks + row_target).astype(jnp.int32).reshape(devices, NT)
    columns = col_target.astype(jnp.int32).reshape(devices, NT, GRP)

    def add_device(carry, inputs):
        dev_blocks, dev_targets, dev_columns, device = inputs
        slab = lax.dynamic_index_in_dim(slabs, device % N_COL, 0, keepdims=False)
        picked = slab[dev_columns].astype(jnp.float32)
        partial_value = jnp.einsum('tgij,tgjk->tik', dev_blocks.astype(jnp.float32), picked, precision=lax.Precision.HIGHEST)
        rounded = lax.optimization_barrier(partial_value.astype(jnp.bfloat16))
        return (carry.at[dev_targets].add(rounded.astype(jnp.float32)), None)
    start = jnp.zeros((RB_DEV * devices, BS, SKETCH), jnp.float32)
    device_ids = jnp.arange(devices, dtype=jnp.int32)
    summed, _ = lax.scan(add_device, start, (blocks, targets, columns, device_ids))
    sketch = summed.reshape(RB_DEV * devices * BS, SKETCH)
    q_factor, r_factor = jnp.linalg.qr(sketch)
    signs = jnp.sign(jnp.diagonal(r_factor))
    q_factor = q_factor * signs[None, :]
    r_factor = r_factor * signs[:, None]
    total = float(RB_DEV * devices * BS)
    basis = (q_factor * jnp.sqrt(total)).astype(jnp.float32)
    factor = (r_factor / jnp.sqrt(total)).astype(jnp.float32)
    return (basis, factor)
```

```python
import functools

import jax
import jax.numpy as jnp
from jax import lax
from jax.experimental import pallas as pl
from jax.experimental.pallas import tpu as pltpu
from jax.sharding import PartitionSpec as P

RB_DEV = 8
CAP = 4
PANEL = 64
MESH = pl.DeviceIdType.MESH
ANY = pl.BlockSpec(memory_space=pl.ANY)
VMEM = pl.BlockSpec(memory_space=pltpu.VMEM)
SMEM = pl.BlockSpec(memory_space=pltpu.SMEM)
HIGH = lax.Precision.HIGHEST


def dot_nn(a, b):
    return lax.dot_general(a, b, (((1,), (0,)), ((), ())), precision=HIGH, preferred_element_type=jnp.float32)


def dot_nt(a, b):
    return lax.dot_general(a, b, (((1,), (1,)), ((), ())), precision=HIGH, preferred_element_type=jnp.float32)


def dot_tn(a, b):
    return lax.dot_general(a, b, (((0,), (0,)), ((), ())), precision=HIGH, preferred_element_type=jnp.float32)


def partial_kernel(slot_ref, col_ref, a_ref, omega_ref, out_ref):
    step = pl.program_id(0)
    per_step, groups, order, _ = a_ref.shape
    for local in range(per_step):
        t = step * per_step + local
        total = None
        for g in range(0, groups, 2):
            left = jnp.concatenate([a_ref[local, g], a_ref[local, g + 1]], axis=1)
            c0 = pl.multiple_of(col_ref[t * groups + g] * order, order)
            c1 = pl.multiple_of(col_ref[t * groups + g + 1] * order, order)
            right = jnp.concatenate([omega_ref[pl.ds(c0, order), :], omega_ref[pl.ds(c1, order), :]], axis=0)
            term = jnp.dot(left, right, preferred_element_type=jnp.float32)
            total = term if total is None else total + term
        out_ref[slot_ref[t]] = total.astype(jnp.bfloat16)


def partials(slot_of, col_flat, a_blocks, omega, slots):
    targets, groups, order, _ = a_blocks.shape
    width = omega.shape[1]
    per_step = 4
    return pl.pallas_call(
        partial_kernel,
        out_shape=jax.ShapeDtypeStruct((slots, order, width), jnp.bfloat16),
        grid_spec=pltpu.PrefetchScalarGridSpec(
            num_scalar_prefetch=2,
            grid=(targets // per_step,),
            in_specs=[
                pl.BlockSpec((per_step, groups, order, order), lambda i, *_: (i, 0, 0, 0)),
                pl.BlockSpec(omega.shape, lambda i, *_: (0, 0)),
            ],
            out_specs=pl.BlockSpec((slots, order, width), lambda i, *_: (0, 0, 0)),
        ),
        compiler_params=pltpu.CompilerParams(vmem_limit_bytes=40 << 20),
    )(slot_of, col_flat, a_blocks, omega)


def row_exchange_kernel(nr, send_ref, srow_ref, got_ref, grow_ref, s_sem, r_sem, s2_sem, r2_sem, own_sem):
    r = lax.axis_index("row")
    c = lax.axis_index("col")
    barrier = pltpu.get_barrier_semaphore()
    for k in range(1, nr):
        pl.semaphore_signal(barrier, inc=1, device_id=(lax.rem(r + k, nr), c), device_id_type=MESH)
    own = pltpu.make_async_copy(send_ref.at[r], got_ref.at[r], own_sem.at[0])
    own_rows = pltpu.make_async_copy(srow_ref.at[r], grow_ref.at[r], own_sem.at[1])
    own.start()
    own_rows.start()
    pl.semaphore_wait(barrier, nr - 1)
    copies = []
    for k in range(1, nr):
        d = lax.rem(r + k, nr)
        for src, dst, ss, rs in ((srow_ref, grow_ref, s2_sem, r2_sem), (send_ref, got_ref, s_sem, r_sem)):
            cp = pltpu.make_async_remote_copy(src.at[d], dst.at[r], ss.at[k], rs.at[k], device_id=(d, c), device_id_type=MESH)
            cp.start()
            copies.append(cp)
    own.wait()
    own_rows.wait()
    for cp in copies:
        cp.wait()


def row_exchange(send, rows, nr):
    dma = pltpu.SemaphoreType.DMA
    return pl.pallas_call(
        functools.partial(row_exchange_kernel, nr),
        out_shape=(jax.ShapeDtypeStruct(send.shape, send.dtype), jax.ShapeDtypeStruct(rows.shape, rows.dtype)),
        in_specs=[ANY, ANY],
        out_specs=(ANY, ANY),
        scratch_shapes=[dma((nr,)), dma((nr,)), dma((nr,)), dma((nr,)), dma((2,))],
        compiler_params=pltpu.CompilerParams(collective_id=1, has_side_effects=True),
    )(send, rows)


def gather_sum_kernel(rows_ref, me_ref, got_ref, term_ref, own_ref, acc):
    acc[...] = jnp.zeros_like(acc)

    @pl.loop(0, got_ref.shape[0])
    def _(s):
        row = rows_ref[s]

        @pl.when(row >= 0)
        def _():
            acc[row] = acc[row] + got_ref[s].astype(jnp.float32)

    @pl.loop(0, acc.shape[0])
    def _(b):
        term_ref[b] = acc[b].astype(jnp.bfloat16)

    @pl.loop(0, own_ref.shape[0])
    def _(b):
        own_ref[b] = acc[me_ref[0] * own_ref.shape[0] + b]


def gather_sum(rows, me, got, blocks):
    _, order, width = got.shape
    return pl.pallas_call(
        gather_sum_kernel,
        out_shape=(
            jax.ShapeDtypeStruct((blocks, order, width), jnp.bfloat16),
            jax.ShapeDtypeStruct((RB_DEV, order, width), jnp.float32),
        ),
        in_specs=[SMEM, SMEM, VMEM],
        out_specs=(VMEM, VMEM),
        scratch_shapes=[pltpu.VMEM((blocks, order, width), jnp.float32)],
        compiler_params=pltpu.CompilerParams(vmem_limit_bytes=48 << 20),
    )(rows, me, got)


def greet(nr, nc, r, c):
    barrier = pltpu.get_barrier_semaphore()
    for k in range(1, nr):
        pl.semaphore_signal(barrier, inc=1, device_id=(lax.rem(r + k, nr), c), device_id_type=MESH)
    for k in range(1, nc):
        pl.semaphore_signal(barrier, inc=1, device_id=(r, lax.rem(c + k, nc)), device_id_type=MESH)
    pl.semaphore_wait(barrier, nr - 1 + nc - 1)


def reduce_gram(nr, nc, r, c, gram, landed, cols, full, sems):
    a_s, a_r, b_s, b_r, c_s, c_r = sems
    chunk = gram.shape[0] // nr
    mine = pl.ds(pl.multiple_of(r * chunk, chunk), chunk)
    copies = []
    for k in range(1, nr):
        d = lax.rem(r + k, nr)
        cp = pltpu.make_async_remote_copy(
            gram.at[pl.ds(pl.multiple_of(d * chunk, chunk), chunk), :], landed.at[k], a_s.at[k], a_r.at[k],
            device_id=(d, c), device_id_type=MESH)
        cp.start()
        copies.append(cp)
    total = gram[mine, :]
    for k in range(1, nr):
        copies[k - 1].wait_recv()
        total = total + landed[k]
    cols[c] = total
    across = []
    for k in range(1, nc):
        cp = pltpu.make_async_remote_copy(
            cols.at[c], cols.at[c], b_s.at[k], b_r.at[k], device_id=(r, lax.rem(c + k, nc)), device_id_type=MESH)
        cp.start()
        across.append(cp)
    for cp in across:
        cp.wait_recv()
    total = cols[0]
    for k in range(1, nc):
        total = total + cols[k]
    full[mine, :] = total
    back = []
    for k in range(1, nr):
        cp = pltpu.make_async_remote_copy(
            full.at[mine, :], full.at[mine, :], c_s.at[k], c_r.at[k], device_id=(lax.rem(r + k, nr), c), device_id_type=MESH)
        cp.start()
        back.append(cp)
    for cp in back:
        cp.wait_recv()
    for cp in copies + across + back:
        cp.wait_send()


def gram_scratch(nr, nc, order):
    dma = pltpu.SemaphoreType.DMA
    chunk = order // nr
    return [
        pltpu.VMEM((nr, chunk, order), jnp.float32),
        pltpu.VMEM((nc, chunk, order), jnp.float32),
        pltpu.VMEM((order, order), jnp.float32),
        dma((nr,)), dma((nr,)), dma((nc,)), dma((nc,)), dma((nr,)), dma((nr,)),
    ]


def col_sum_kernel(nr, nc, term_ref, own_ref, sketch_ref, out_ref, got, gram, landed, cols, full, *sems):
    r = lax.axis_index("row")
    c = lax.axis_index("col")
    s_sem, r_sem = sems[6], sems[7]
    greet(nr, nc, r, c)
    copies = []
    for k in range(1, nc):
        d = lax.rem(c + k, nc)
        cp = pltpu.make_async_remote_copy(
            term_ref.at[pl.ds(d * RB_DEV, RB_DEV)], got.at[k], s_sem.at[k], r_sem.at[k],
            device_id=(r, d), device_id_type=MESH)
        cp.start()
        copies.append(cp)
    for cp in copies:
        cp.wait()
    order = own_ref.shape[1]
    gram[...] = jnp.zeros_like(gram)

    @pl.loop(0, RB_DEV // 2)
    def _(i):
        pieces = []
        for half in range(2):
            b = i * 2 + half
            total = own_ref[b]
            for k in range(1, nc):
                total = total + got[k, b].astype(jnp.float32)
            pieces.append(total)
        rows = jnp.concatenate(pieces, axis=0)
        sketch_ref[pl.ds(pl.multiple_of(i * 2 * order, 2 * order), 2 * order), :] = rows
        gram[...] += dot_tn(rows, rows)

    reduce_gram(nr, nc, r, c, gram, landed, cols, full, sems[:6])
    out_ref[...] = full[...]


def col_sum(term, own, nr, nc):
    _, order, width = own.shape
    dma = pltpu.SemaphoreType.DMA
    return pl.pallas_call(
        functools.partial(col_sum_kernel, nr, nc),
        out_shape=(
            jax.ShapeDtypeStruct((RB_DEV * order, width), jnp.float32),
            jax.ShapeDtypeStruct((width, width), jnp.float32),
        ),
        in_specs=[VMEM, VMEM],
        out_specs=(VMEM, VMEM),
        scratch_shapes=[
            pltpu.VMEM((nc, RB_DEV, order, width), jnp.bfloat16),
            pltpu.VMEM((width, width), jnp.float32),
        ] + gram_scratch(nr, nc, width) + [dma((nc,)), dma((nc,))],
        compiler_params=pltpu.CompilerParams(collective_id=2, has_side_effects=True, vmem_limit_bytes=48 << 20),
    )(term, own)


def gram_sum_kernel(nr, nc, gram, out_ref, landed, cols, full, *sems):
    r = lax.axis_index("row")
    c = lax.axis_index("col")
    greet(nr, nc, r, c)
    reduce_gram(nr, nc, r, c, gram, landed, cols, full, sems)
    out_ref[...] = full[...]


def gram_sum(gram, nr, nc):
    return pl.pallas_call(
        functools.partial(gram_sum_kernel, nr, nc),
        out_shape=jax.ShapeDtypeStruct(gram.shape, jnp.float32),
        in_specs=[VMEM],
        out_specs=VMEM,
        scratch_shapes=gram_scratch(nr, nc, gram.shape[0]),
        compiler_params=pltpu.CompilerParams(collective_id=3, has_side_effects=True),
    )(gram)


def eliminate(x):
    rows = x.shape[0]
    groups = [x[i:i + 8, :] for i in range(0, rows, 8)]
    sub = lax.broadcasted_iota(jnp.int32, (8, 1), 0)
    for j in range(rows - 1):
        g, o = divmod(j, 8)
        pivot_row = groups[g][o:o + 1, :]
        scaled = pivot_row * (1.0 / pivot_row[:, j:j + 1])
        for i in range(g, rows // 8):
            f = groups[i][:, j:j + 1]
            if i == g:
                if o == 7:
                    continue
                f = jnp.where(sub > o, f, 0.0)
            groups[i] = groups[i] - f * scaled
    return jnp.concatenate(groups, axis=0)


def factor_gram(gram, work, upper, inverse):
    order = gram.shape[0]
    row = lax.broadcasted_iota(jnp.int32, (order, order), 0)
    col = lax.broadcasted_iota(jnp.int32, (order, order), 1)
    work[:, :order] = gram[...]
    work[:, order:] = (row == col).astype(jnp.float32)
    lane = lax.broadcasted_iota(jnp.int32, (PANEL, 2 * PANEL), 1)
    prow = lax.broadcasted_iota(jnp.int32, (PANEL, 2 * PANEL), 0)

    @pl.loop(0, order // PANEL)
    def _(p):
        base = pl.multiple_of(p * PANEL, PANEL)
        tile = work[pl.ds(base, PANEL), pl.ds(pl.multiple_of((p // 2) * 2 * PANEL, 2 * PANEL), 2 * PANEL)]
        tile = jnp.where(p % 2 == 1, pltpu.roll(tile, PANEL, 1), tile)
        x = jnp.where(lane < PANEL, tile, (lane - PANEL == prow).astype(jnp.float32))
        x = eliminate(x)
        diag = jnp.sum(jnp.where(lane == prow, x, 0.0), axis=1, keepdims=True)
        left = pltpu.roll(x, PANEL, 1)[:, :PANEL]
        panel = dot_nn(left, work[pl.ds(base, PANEL), :])
        root = 1.0 / jnp.sqrt(diag)
        pcol = lax.broadcasted_iota(jnp.int32, (PANEL, order), 1)
        pr = lax.broadcasted_iota(jnp.int32, (PANEL, order), 0) + base
        upper[pl.ds(base, PANEL), :] = jnp.where(pcol >= pr, panel[:, :order] * root, 0.0)
        inverse[pl.ds(base, PANEL), :] = jnp.where(pcol <= pr, panel[:, order:] * root, 0.0)

        @pl.when(p < order // PANEL - 1)
        def _():
            half = panel * root
            update = dot_tn(half[:, :order], half)
            below = lax.broadcasted_iota(jnp.int32, (order, 1), 0) >= base + PANEL
            work[...] = jnp.where(below, work[...] - update, work[...])


def first_kernel(gram, sketch, upper, once, second, work, inverse):
    factor_gram(gram, work, upper, inverse)
    second[...] = jnp.zeros_like(second)
    step = 256

    @pl.loop(0, sketch.shape[0] // step)
    def _(i):
        part = pl.ds(pl.multiple_of(i * step, step), step)
        rows = dot_nt(sketch[part, :], inverse[...])
        once[part, :] = rows
        second[...] += dot_tn(rows, rows)


def first_pass(gram, sketch):
    order = gram.shape[0]
    square = jax.ShapeDtypeStruct((order, order), jnp.float32)
    return pl.pallas_call(
        first_kernel,
        out_shape=(square, jax.ShapeDtypeStruct(sketch.shape, jnp.float32), square),
        in_specs=[VMEM, VMEM],
        out_specs=(VMEM, VMEM, VMEM),
        scratch_shapes=[pltpu.VMEM((order, 2 * order), jnp.float32), pltpu.VMEM((order, order), jnp.float32)],
        compiler_params=pltpu.CompilerParams(vmem_limit_bytes=40 << 20),
    )(gram, sketch)


def last_kernel(scale, gram, once, upper_one, basis, factor, work, upper, inverse):
    factor_gram(gram, work, upper, inverse)
    factor[...] = dot_nn(upper[...], upper_one[...]) * (1.0 / scale)
    step = 256

    @pl.loop(0, once.shape[0] // step)
    def _(i):
        part = pl.ds(pl.multiple_of(i * step, step), step)
        basis[part, :] = dot_nt(once[part, :], inverse[...]) * scale


def last_pass(gram, once, upper_one, scale):
    order = gram.shape[0]
    square = pltpu.VMEM((order, order), jnp.float32)
    return pl.pallas_call(
        functools.partial(last_kernel, scale),
        out_shape=(
            jax.ShapeDtypeStruct(once.shape, jnp.float32),
            jax.ShapeDtypeStruct((order, order), jnp.float32),
        ),
        in_specs=[VMEM, VMEM, VMEM],
        out_specs=(VMEM, VMEM),
        scratch_shapes=[pltpu.VMEM((order, 2 * order), jnp.float32), square, square],
        compiler_params=pltpu.CompilerParams(vmem_limit_bytes=40 << 20),
    )(gram, once, upper_one)


def body(nr, nc, a_blocks, omega, route_dest, row_target, col_target):
    targets_here, _, order, _ = a_blocks.shape
    width = omega.shape[1]
    slots = nr * CAP
    destination = route_dest[:, 0]
    positions = jnp.arange(targets_here, dtype=jnp.int32)
    same_owner = destination[:, None] == destination[None, :]
    earlier = positions[None, :] < positions[:, None]
    rank = jnp.sum(jnp.logical_and(same_owner, earlier).astype(jnp.int32), axis=1)
    slot_of = destination * CAP + rank
    slot_ids = jnp.arange(slots, dtype=jnp.int32)
    matches = slot_of[None, :] == slot_ids[:, None]
    send_rows = jnp.sum(jnp.where(matches, row_target[None, :] + 1, 0), axis=1) - 1
    send_rows = jnp.pad(send_rows.reshape(nr, 1, CAP), ((0, 0), (0, 0), (0, 128 - CAP)))
    send_rows = jnp.broadcast_to(send_rows, (nr, 8, 128))
    send = partials(slot_of, col_target.reshape(-1), a_blocks, omega, slots)
    got, got_rows = row_exchange(send.reshape(nr, CAP, order, width), send_rows, nr)
    me = lax.axis_index("col").astype(jnp.int32).reshape(1)
    term, own = gather_sum(got_rows[:, 0, :CAP].reshape(slots), me, got.reshape(slots, order, width), nc * RB_DEV)
    sketch, gram_one = col_sum(term, own, nr, nc)
    upper_one, once, gram_part = first_pass(gram_one, sketch)
    gram_two = gram_sum(gram_part, nr, nc)
    scale = float(nr * nc * RB_DEV * order) ** 0.5
    return last_pass(gram_two, once, upper_one, scale)


def solution(mesh):
    nr, nc = mesh.shape["row"], mesh.shape["col"]
    return jax.shard_map(
        functools.partial(body, nr, nc),
        mesh=mesh,
        in_specs=(
            P(("row", "col"), None, None, None),
            P("col", None),
            P(("row", "col"), None),
            P(("row", "col")),
            P(("row", "col"), None),
        ),
        out_specs=(P(("row", "col"), None), P()),
        check_vma=False,
    )
```

```python
import functools

import jax
import jax.numpy as jnp
from jax import lax
from jax.experimental import pallas as pl
from jax.experimental.pallas import tpu as pltpu
from jax.sharding import PartitionSpec as P

RB_DEV = 8
CAP = 4
PANEL = 64
HALVES = 2
WIDE = 4
MESH = pl.DeviceIdType.MESH
ANY = pl.BlockSpec(memory_space=pl.ANY)
VMEM = pl.BlockSpec(memory_space=pltpu.VMEM)
SMEM = pl.BlockSpec(memory_space=pltpu.SMEM)
HIGH = lax.Precision.HIGHEST


def dot_nn(a, b):
    return lax.dot_general(a, b, (((1,), (0,)), ((), ())), precision=HIGH, preferred_element_type=jnp.float32)


def dot_nt(a, b):
    return lax.dot_general(a, b, (((1,), (1,)), ((), ())), precision=HIGH, preferred_element_type=jnp.float32)


def dot_tn(a, b):
    return lax.dot_general(a, b, (((0,), (0,)), ((), ())), precision=HIGH, preferred_element_type=jnp.float32)


def partial_kernel(slot_ref, col_ref, a_ref, omega_ref, out_ref):
    step = pl.program_id(0)
    per_step, groups, order, _ = a_ref.shape
    for local in range(per_step):
        t = step * per_step + local
        total = None
        for g in range(0, groups, 2):
            left = jnp.concatenate([a_ref[local, g], a_ref[local, g + 1]], axis=1)
            c0 = pl.multiple_of(col_ref[t * groups + g] * order, order)
            c1 = pl.multiple_of(col_ref[t * groups + g + 1] * order, order)
            right = jnp.concatenate([omega_ref[pl.ds(c0, order), :], omega_ref[pl.ds(c1, order), :]], axis=0)
            term = jnp.dot(left, right, preferred_element_type=jnp.float32)
            total = term if total is None else total + term
        total = total.astype(jnp.bfloat16)
        half = out_ref.shape[-1]
        for h in range(HALVES):
            out_ref[h, slot_ref[t]] = total[:, h * half:(h + 1) * half]


def partials(slot_of, col_flat, a_blocks, omega, slots):
    targets, groups, order, _ = a_blocks.shape
    width = omega.shape[1]
    per_step = 4
    return pl.pallas_call(
        partial_kernel,
        out_shape=jax.ShapeDtypeStruct((HALVES, slots, order, width // HALVES), jnp.bfloat16),
        grid_spec=pltpu.PrefetchScalarGridSpec(
            num_scalar_prefetch=2,
            grid=(targets // per_step,),
            in_specs=[
                pl.BlockSpec((per_step, groups, order, order), lambda i, *_: (i, 0, 0, 0)),
                pl.BlockSpec(omega.shape, lambda i, *_: (0, 0)),
            ],
            out_specs=pl.BlockSpec((HALVES, slots, order, width // HALVES), lambda i, *_: (0, 0, 0, 0)),
        ),
        compiler_params=pltpu.CompilerParams(vmem_limit_bytes=40 << 20),
    )(slot_of, col_flat, a_blocks, omega)


def row_exchange_kernel(nr, send_ref, srow_ref, got_ref, grow_ref, s_sem, r_sem, s2_sem, r2_sem, own_sem):
    r = lax.axis_index("row")
    c = lax.axis_index("col")
    barrier = pltpu.get_barrier_semaphore()
    for k in range(1, nr):
        pl.semaphore_signal(barrier, inc=1, device_id=(lax.rem(r + k, nr), c), device_id_type=MESH)
    own = pltpu.make_async_copy(send_ref.at[0, r], got_ref.at[r], own_sem.at[0])
    own_rows = pltpu.make_async_copy(srow_ref.at[r], grow_ref.at[r], own_sem.at[1])
    own.start()
    own_rows.start()
    pl.semaphore_wait(barrier, nr - 1)
    copies = []
    for k in range(1, nr):
        d = lax.rem(r + k, nr)
        for src, dst, ss, rs in ((srow_ref, grow_ref, s2_sem, r2_sem), (send_ref.at[0], got_ref, s_sem, r_sem)):
            cp = pltpu.make_async_remote_copy(src.at[d], dst.at[r], ss.at[k], rs.at[k], device_id=(d, c), device_id_type=MESH)
            cp.start()
            copies.append(cp)
    own.wait()
    own_rows.wait()
    for cp in copies:
        cp.wait()


def row_exchange(send, rows, nr):
    dma = pltpu.SemaphoreType.DMA
    return pl.pallas_call(
        functools.partial(row_exchange_kernel, nr),
        out_shape=(jax.ShapeDtypeStruct(send.shape[1:], send.dtype), jax.ShapeDtypeStruct(rows.shape, rows.dtype)),
        in_specs=[ANY, ANY],
        out_specs=(ANY, ANY),
        scratch_shapes=[dma((nr,)), dma((nr,)), dma((nr,)), dma((nr,)), dma((2,))],
        compiler_params=pltpu.CompilerParams(collective_id=1, has_side_effects=True),
    )(send, rows)


def both_exchange_kernel(nr, nc, send_ref, term_ref, got_ref, arrived_ref, s_sem, r_sem, s2_sem, r2_sem, own_sem):
    r = lax.axis_index("row")
    c = lax.axis_index("col")
    own = pltpu.make_async_copy(send_ref.at[1, r], got_ref.at[r], own_sem.at[0])
    own.start()
    greet(nr, nc, r, c)
    copies = []
    for k in range(1, nc):
        d = lax.rem(c + k, nc)
        copies.append(pltpu.make_async_remote_copy(
            term_ref.at[pl.ds(d * RB_DEV, RB_DEV)], arrived_ref.at[k], s2_sem.at[k], r2_sem.at[k],
            device_id=(r, d), device_id_type=MESH))
        copies[-1].start()
    for k in range(1, nr):
        d = lax.rem(r + k, nr)
        copies.append(pltpu.make_async_remote_copy(
            send_ref.at[1, d], got_ref.at[r], s_sem.at[k], r_sem.at[k], device_id=(d, c), device_id_type=MESH))
        copies[-1].start()
    own.wait()
    for cp in copies:
        cp.wait()


def both_exchange(send, term, nr, nc):
    dma = pltpu.SemaphoreType.DMA
    _, order, width = term.shape
    return pl.pallas_call(
        functools.partial(both_exchange_kernel, nr, nc),
        out_shape=(
            jax.ShapeDtypeStruct(send.shape[1:], send.dtype),
            jax.ShapeDtypeStruct((nc, RB_DEV, order, width), term.dtype),
        ),
        in_specs=[ANY, ANY],
        out_specs=(ANY, ANY),
        scratch_shapes=[dma((nr,)), dma((nr,)), dma((nc,)), dma((nc,)), dma((1,))],
        compiler_params=pltpu.CompilerParams(collective_id=4, has_side_effects=True),
    )(send, term)


def gather_sum_kernel(rows_ref, me_ref, got_ref, term_ref, own_ref, acc):
    acc[...] = jnp.zeros_like(acc)

    @pl.loop(0, got_ref.shape[0])
    def _(s):
        row = rows_ref[s]

        @pl.when(row >= 0)
        def _():
            acc[row] = acc[row] + got_ref[s].astype(jnp.float32)

    @pl.loop(0, acc.shape[0])
    def _(b):
        term_ref[b] = acc[b].astype(jnp.bfloat16)

    @pl.loop(0, own_ref.shape[0])
    def _(b):
        own_ref[b] = acc[me_ref[0] * own_ref.shape[0] + b]


def gather_sum(rows, me, got, blocks):
    _, order, width = got.shape
    return pl.pallas_call(
        gather_sum_kernel,
        out_shape=(
            jax.ShapeDtypeStruct((blocks, order, width), jnp.bfloat16),
            jax.ShapeDtypeStruct((RB_DEV, order, width), jnp.float32),
        ),
        in_specs=[SMEM, SMEM, VMEM],
        out_specs=(VMEM, VMEM),
        scratch_shapes=[pltpu.VMEM((blocks, order, width), jnp.float32)],
        compiler_params=pltpu.CompilerParams(vmem_limit_bytes=48 << 20),
    )(rows, me, got)


def greet(nr, nc, r, c):
    barrier = pltpu.get_barrier_semaphore()
    for k in range(1, nr):
        pl.semaphore_signal(barrier, inc=1, device_id=(lax.rem(r + k, nr), c), device_id_type=MESH)
    for k in range(1, nc):
        pl.semaphore_signal(barrier, inc=1, device_id=(r, lax.rem(c + k, nc)), device_id_type=MESH)
    pl.semaphore_wait(barrier, nr - 1 + nc - 1)


def reduce_gram(nr, nc, r, c, gram, landed, cols, full, sems):
    a_s, a_r, b_s, b_r, c_s, c_r = sems
    chunk = gram.shape[0] // nr
    mine = pl.ds(pl.multiple_of(r * chunk, chunk), chunk)
    copies = []
    for k in range(1, nr):
        d = lax.rem(r + k, nr)
        cp = pltpu.make_async_remote_copy(
            gram.at[pl.ds(pl.multiple_of(d * chunk, chunk), chunk), :], landed.at[k], a_s.at[k], a_r.at[k],
            device_id=(d, c), device_id_type=MESH)
        cp.start()
        copies.append(cp)
    total = gram[mine, :]
    for k in range(1, nr):
        copies[k - 1].wait_recv()
        total = total + landed[k]
    cols[c] = total
    across = []
    for k in range(1, nc):
        cp = pltpu.make_async_remote_copy(
            cols.at[c], cols.at[c], b_s.at[k], b_r.at[k], device_id=(r, lax.rem(c + k, nc)), device_id_type=MESH)
        cp.start()
        across.append(cp)
    for cp in across:
        cp.wait_recv()
    total = cols[0]
    for k in range(1, nc):
        total = total + cols[k]
    full[mine, :] = total
    back = []
    for k in range(1, nr):
        cp = pltpu.make_async_remote_copy(
            full.at[mine, :], full.at[mine, :], c_s.at[k], c_r.at[k], device_id=(lax.rem(r + k, nr), c), device_id_type=MESH)
        cp.start()
        back.append(cp)
    for cp in back:
        cp.wait_recv()
    for cp in copies + across + back:
        cp.wait_send()


def gram_scratch(nr, nc, order):
    dma = pltpu.SemaphoreType.DMA
    chunk = order // nr
    return [
        pltpu.VMEM((nr, chunk, order), jnp.float32),
        pltpu.VMEM((nc, chunk, order), jnp.float32),
        pltpu.VMEM((order, order), jnp.float32),
        dma((nr,)), dma((nr,)), dma((nc,)), dma((nc,)), dma((nr,)), dma((nr,)),
    ]


def col_sum_kernel(nr, nc, term_ref, own_ref, arrived0, own0, sketch_ref, out_ref, got, gram, landed, cols, full, *sems):
    r = lax.axis_index("row")
    c = lax.axis_index("col")
    s_sem, r_sem = sems[6], sems[7]
    greet(nr, nc, r, c)
    copies = []
    for k in range(1, nc):
        d = lax.rem(c + k, nc)
        cp = pltpu.make_async_remote_copy(
            term_ref.at[pl.ds(d * RB_DEV, RB_DEV)], got.at[k], s_sem.at[k], r_sem.at[k],
            device_id=(r, d), device_id_type=MESH)
        cp.start()
        copies.append(cp)
    for cp in copies:
        cp.wait()
    order = own_ref.shape[1]
    gram[...] = jnp.zeros_like(gram)

    @pl.loop(0, RB_DEV // 2)
    def _(i):
        pieces = []
        for half in range(2):
            b = i * 2 + half
            total0, total1 = own0[b], own_ref[b]
            for k in range(1, nc):
                total0 = total0 + arrived0[k, b].astype(jnp.float32)
                total1 = total1 + got[k, b].astype(jnp.float32)
            pieces.append(jnp.concatenate([total0, total1], axis=1))
        rows = jnp.concatenate(pieces, axis=0)
        sketch_ref[pl.ds(pl.multiple_of(i * 2 * order, 2 * order), 2 * order), :] = rows
        gram[...] += dot_tn(rows, rows)

    reduce_gram(nr, nc, r, c, gram, landed, cols, full, sems[:6])
    out_ref[...] = full[...]


def col_sum(term, own, arrived0, own0, nr, nc):
    _, order, half = own.shape
    width = HALVES * half
    dma = pltpu.SemaphoreType.DMA
    return pl.pallas_call(
        functools.partial(col_sum_kernel, nr, nc),
        out_shape=(
            jax.ShapeDtypeStruct((RB_DEV * order, width), jnp.float32),
            jax.ShapeDtypeStruct((width, width), jnp.float32),
        ),
        in_specs=[VMEM, VMEM, VMEM, VMEM],
        out_specs=(VMEM, VMEM),
        scratch_shapes=[
            pltpu.VMEM((nc, RB_DEV, order, half), jnp.bfloat16),
            pltpu.VMEM((width, width), jnp.float32),
        ] + gram_scratch(nr, nc, width) + [dma((nc,)), dma((nc,))],
        compiler_params=pltpu.CompilerParams(collective_id=2, has_side_effects=True, vmem_limit_bytes=48 << 20),
    )(term, own, arrived0, own0)


def gram_sum_kernel(nr, nc, gram, out_ref, landed, cols, full, *sems):
    r = lax.axis_index("row")
    c = lax.axis_index("col")
    greet(nr, nc, r, c)
    reduce_gram(nr, nc, r, c, gram, landed, cols, full, sems)
    out_ref[...] = full[...]


def gram_sum(gram, nr, nc):
    return pl.pallas_call(
        functools.partial(gram_sum_kernel, nr, nc),
        out_shape=jax.ShapeDtypeStruct(gram.shape, jnp.float32),
        in_specs=[VMEM],
        out_specs=VMEM,
        scratch_shapes=gram_scratch(nr, nc, gram.shape[0]),
        compiler_params=pltpu.CompilerParams(collective_id=3, has_side_effects=True),
    )(gram)


def eliminate(x):
    rows = x.shape[0]
    shape = (8, x.shape[1])
    groups = [x[i:i + 8, :] for i in range(0, rows, 8)]
    sub = lax.broadcasted_iota(jnp.int32, shape, 0)
    for j in range(0, rows, WIDE):
        g, o = divmod(j, 8)
        cols = [[jnp.broadcast_to(groups[i][:, j + l:j + l + 1], shape) for l in range(WIDE)]
                for i in range(g, rows // 8)]
        piv = [[jnp.broadcast_to(cols[0][l][o + k:o + k + 1, :], shape) for l in range(WIDE)] for k in range(WIDE)]
        tops = [jnp.broadcast_to(groups[g][o + k:o + k + 1, :], shape) for k in range(WIDE)]
        recip = []
        for k in range(WIDE):
            recip.append(1.0 / piv[k][k])
            for m in range(k + 1, WIDE):
                q = piv[m][k] * recip[k]
                for l in range(k + 1, WIDE):
                    piv[m][l] = piv[m][l] - q * piv[k][l]
                tops[m] = tops[m] - q * tops[k]
        for i in range(g, rows // 8):
            here = cols[i - g]
            value = groups[i]
            for k in range(WIDE):
                f = here[k] * recip[k]
                for l in range(k + 1, WIDE):
                    here[l] = here[l] - f * piv[k][l]
                value = value - f * tops[k]
            if i == g:
                value = jnp.where(sub >= o + WIDE, value, groups[i])
                for k in range(1, WIDE):
                    value = jnp.where(sub == o + k, tops[k], value)
            groups[i] = value
    return jnp.concatenate(groups, axis=0)


def factor_gram(gram, work, upper, inverse):
    order = gram.shape[0]
    row = lax.broadcasted_iota(jnp.int32, (order, order), 0)
    col = lax.broadcasted_iota(jnp.int32, (order, order), 1)
    work[:, :order] = gram[...]
    work[:, order:] = (row == col).astype(jnp.float32)
    lane = lax.broadcasted_iota(jnp.int32, (PANEL, 2 * PANEL), 1)
    prow = lax.broadcasted_iota(jnp.int32, (PANEL, 2 * PANEL), 0)

    @pl.loop(0, order // PANEL)
    def _(p):
        base = pl.multiple_of(p * PANEL, PANEL)
        tile = work[pl.ds(base, PANEL), pl.ds(pl.multiple_of((p // 2) * 2 * PANEL, 2 * PANEL), 2 * PANEL)]
        tile = jnp.where(p % 2 == 1, pltpu.roll(tile, PANEL, 1), tile)
        x = jnp.where(lane < PANEL, tile, (lane - PANEL == prow).astype(jnp.float32))
        x = eliminate(x)
        diag = jnp.sum(jnp.where(lane == prow, x, 0.0), axis=1, keepdims=True)
        left = pltpu.roll(x, PANEL, 1)[:, :PANEL]
        panel = dot_nn(left, work[pl.ds(base, PANEL), :])
        root = 1.0 / jnp.sqrt(diag)
        pcol = lax.broadcasted_iota(jnp.int32, (PANEL, order), 1)
        pr = lax.broadcasted_iota(jnp.int32, (PANEL, order), 0) + base
        upper[pl.ds(base, PANEL), :] = jnp.where(pcol >= pr, panel[:, :order] * root, 0.0)
        inverse[pl.ds(base, PANEL), :] = jnp.where(pcol <= pr, panel[:, order:] * root, 0.0)

        @pl.when(p < order // PANEL - 1)
        def _():
            half = panel * root
            update = dot_tn(half[:, :order], half)
            below = lax.broadcasted_iota(jnp.int32, (order, 1), 0) >= base + PANEL
            work[...] = jnp.where(below, work[...] - update, work[...])


def first_kernel(gram, sketch, upper, once, second, work, inverse):
    factor_gram(gram, work, upper, inverse)
    second[...] = jnp.zeros_like(second)
    step = 256

    @pl.loop(0, sketch.shape[0] // step)
    def _(i):
        part = pl.ds(pl.multiple_of(i * step, step), step)
        rows = dot_nt(sketch[part, :], inverse[...])
        once[part, :] = rows
        second[...] += dot_tn(rows, rows)


def first_pass(gram, sketch):
    order = gram.shape[0]
    square = jax.ShapeDtypeStruct((order, order), jnp.float32)
    return pl.pallas_call(
        first_kernel,
        out_shape=(square, jax.ShapeDtypeStruct(sketch.shape, jnp.float32), square),
        in_specs=[VMEM, VMEM],
        out_specs=(VMEM, VMEM, VMEM),
        scratch_shapes=[pltpu.VMEM((order, 2 * order), jnp.float32), pltpu.VMEM((order, order), jnp.float32)],
        compiler_params=pltpu.CompilerParams(vmem_limit_bytes=40 << 20),
    )(gram, sketch)


def last_kernel(scale, gram, once, upper_one, basis, factor, work, upper, inverse):
    factor_gram(gram, work, upper, inverse)
    factor[...] = dot_nn(upper[...], upper_one[...]) * (1.0 / scale)
    step = 256

    @pl.loop(0, once.shape[0] // step)
    def _(i):
        part = pl.ds(pl.multiple_of(i * step, step), step)
        basis[part, :] = dot_nt(once[part, :], inverse[...]) * scale


def last_pass(gram, once, upper_one, scale):
    order = gram.shape[0]
    square = pltpu.VMEM((order, order), jnp.float32)
    return pl.pallas_call(
        functools.partial(last_kernel, scale),
        out_shape=(
            jax.ShapeDtypeStruct(once.shape, jnp.float32),
            jax.ShapeDtypeStruct((order, order), jnp.float32),
        ),
        in_specs=[VMEM, VMEM, VMEM],
        out_specs=(VMEM, VMEM),
        scratch_shapes=[pltpu.VMEM((order, 2 * order), jnp.float32), square, square],
        compiler_params=pltpu.CompilerParams(vmem_limit_bytes=40 << 20),
    )(gram, once, upper_one)


def body(nr, nc, a_blocks, omega, route_dest, row_target, col_target):
    targets_here, _, order, _ = a_blocks.shape
    width = omega.shape[1]
    slots = nr * CAP
    destination = route_dest[:, 0]
    positions = jnp.arange(targets_here, dtype=jnp.int32)
    same_owner = destination[:, None] == destination[None, :]
    earlier = positions[None, :] < positions[:, None]
    rank = jnp.sum(jnp.logical_and(same_owner, earlier).astype(jnp.int32), axis=1)
    slot_of = destination * CAP + rank
    slot_ids = jnp.arange(slots, dtype=jnp.int32)
    matches = slot_of[None, :] == slot_ids[:, None]
    send_rows = jnp.sum(jnp.where(matches, row_target[None, :] + 1, 0), axis=1) - 1
    send_rows = jnp.pad(send_rows.reshape(nr, 1, CAP), ((0, 0), (0, 0), (0, 128 - CAP)))
    send_rows = jnp.broadcast_to(send_rows, (nr, 8, 128))
    send = partials(slot_of, col_target.reshape(-1), a_blocks, omega, slots)
    half = width // HALVES
    send = send.reshape(HALVES, nr, CAP, order, half)
    got0, got_rows = row_exchange(send, send_rows, nr)
    me = lax.axis_index("col").astype(jnp.int32).reshape(1)
    rows = got_rows[:, 0, :CAP].reshape(slots)
    term0, own0 = gather_sum(rows, me, got0.reshape(slots, order, half), nc * RB_DEV)
    got1, arrived0 = both_exchange(send, term0, nr, nc)
    term1, own1 = gather_sum(rows, me, got1.reshape(slots, order, half), nc * RB_DEV)
    sketch, gram_one = col_sum(term1, own1, arrived0, own0, nr, nc)
    upper_one, once, gram_part = first_pass(gram_one, sketch)
    gram_two = gram_sum(gram_part, nr, nc)
    scale = float(nr * nc * RB_DEV * order) ** 0.5
    return last_pass(gram_two, once, upper_one, scale)


def solution(mesh):
    nr, nc = mesh.shape["row"], mesh.shape["col"]
    return jax.shard_map(
        functools.partial(body, nr, nc),
        mesh=mesh,
        in_specs=(
            P(("row", "col"), None, None, None),
            P("col", None),
            P(("row", "col"), None),
            P(("row", "col")),
            P(("row", "col"), None),
        ),
        out_specs=(P(("row", "col"), None), P()),
        check_vma=False,
    )
```

```python
import functools

import jax
import jax.numpy as jnp
from jax import lax
from jax.experimental import pallas as pl
from jax.experimental.pallas import tpu as pltpu
from jax.sharding import PartitionSpec as P

RB_DEV = 8
CAP = 4
PANEL = 64
HALVES = 2
WIDE = 4
MESH = pl.DeviceIdType.MESH
VMEM = pl.BlockSpec(memory_space=pltpu.VMEM)
SMEM = pl.BlockSpec(memory_space=pltpu.SMEM)
HIGH = lax.Precision.HIGHEST


def dot_nn(a, b):
    return lax.dot_general(a, b, (((1,), (0,)), ((), ())), precision=HIGH, preferred_element_type=jnp.float32)


def dot_nt(a, b):
    return lax.dot_general(a, b, (((1,), (1,)), ((), ())), precision=HIGH, preferred_element_type=jnp.float32)


def dot_tn(a, b):
    return lax.dot_general(a, b, (((0,), (0,)), ((), ())), precision=HIGH, preferred_element_type=jnp.float32)


def partial_kernel(slot_ref, col_ref, a_ref, omega_ref, out_ref):
    step = pl.program_id(0)
    per_step, groups, order, _ = a_ref.shape
    for local in range(per_step):
        t = step * per_step + local
        total = None
        for g in range(0, groups, 2):
            left = jnp.concatenate([a_ref[local, g], a_ref[local, g + 1]], axis=1)
            c0 = pl.multiple_of(col_ref[t * groups + g] * order, order)
            c1 = pl.multiple_of(col_ref[t * groups + g + 1] * order, order)
            right = jnp.concatenate([omega_ref[pl.ds(c0, order), :], omega_ref[pl.ds(c1, order), :]], axis=0)
            term = jnp.dot(left, right, preferred_element_type=jnp.float32)
            total = term if total is None else total + term
        total = total.astype(jnp.bfloat16)
        half = out_ref.shape[-1]
        for h in range(HALVES):
            out_ref[h, slot_ref[t]] = total[:, h * half:(h + 1) * half]


def partials(slot_of, col_flat, a_blocks, omega, slots):
    targets, groups, order, _ = a_blocks.shape
    width = omega.shape[1]
    per_step = 4
    return pl.pallas_call(
        partial_kernel,
        out_shape=jax.ShapeDtypeStruct((HALVES, slots, order, width // HALVES), jnp.bfloat16),
        grid_spec=pltpu.PrefetchScalarGridSpec(
            num_scalar_prefetch=2,
            grid=(targets // per_step,),
            in_specs=[
                pl.BlockSpec((per_step, groups, order, order), lambda i, *_: (i, 0, 0, 0)),
                pl.BlockSpec(omega.shape, lambda i, *_: (0, 0)),
            ],
            out_specs=pl.BlockSpec((HALVES, slots, order, width // HALVES), lambda i, *_: (0, 0, 0, 0)),
        ),
        compiler_params=pltpu.CompilerParams(vmem_limit_bytes=50 << 20),
    )(slot_of, col_flat, a_blocks, omega)


def row_exchange_kernel(nr, send_ref, srow_ref, got_ref, grow_ref, s_sem, r_sem, s2_sem, r2_sem, own_sem):
    r = lax.axis_index("row")
    c = lax.axis_index("col")
    barrier = pltpu.get_barrier_semaphore()
    for k in range(1, nr):
        pl.semaphore_signal(barrier, inc=1, device_id=(lax.rem(r + k, nr), c), device_id_type=MESH)
    own = pltpu.make_async_copy(send_ref.at[0, r], got_ref.at[r], own_sem.at[0])
    own_rows = pltpu.make_async_copy(srow_ref.at[r], grow_ref.at[r], own_sem.at[1])
    own.start()
    own_rows.start()
    pl.semaphore_wait(barrier, nr - 1)
    copies = []
    for k in range(1, nr):
        d = lax.rem(r + k, nr)
        for src, dst, ss, rs in ((srow_ref, grow_ref, s2_sem, r2_sem), (send_ref.at[0], got_ref, s_sem, r_sem)):
            cp = pltpu.make_async_remote_copy(src.at[d], dst.at[r], ss.at[k], rs.at[k], device_id=(d, c), device_id_type=MESH)
            cp.start()
            copies.append(cp)
    own.wait()
    own_rows.wait()
    for cp in copies:
        cp.wait()


def row_exchange(send, rows, nr):
    dma = pltpu.SemaphoreType.DMA
    return pl.pallas_call(
        functools.partial(row_exchange_kernel, nr),
        out_shape=(jax.ShapeDtypeStruct(send.shape[1:], send.dtype), jax.ShapeDtypeStruct(rows.shape, rows.dtype)),
        in_specs=[VMEM, VMEM],
        out_specs=(VMEM, VMEM),
        scratch_shapes=[dma((nr,)), dma((nr,)), dma((nr,)), dma((nr,)), dma((2,))],
        compiler_params=pltpu.CompilerParams(collective_id=1, has_side_effects=True, vmem_limit_bytes=16 << 20),
    )(send, rows)


def both_exchange_kernel(nr, nc, send_ref, term_ref, got_ref, arrived_ref, s_sem, r_sem, s2_sem, r2_sem, own_sem):
    r = lax.axis_index("row")
    c = lax.axis_index("col")
    own = pltpu.make_async_copy(send_ref.at[1, r], got_ref.at[r], own_sem.at[0])
    own.start()
    greet(nr, nc, r, c)
    copies = []
    for k in range(1, nc):
        d = lax.rem(c + k, nc)
        copies.append(pltpu.make_async_remote_copy(
            term_ref.at[pl.ds(d * RB_DEV, RB_DEV)], arrived_ref.at[k], s2_sem.at[k], r2_sem.at[k],
            device_id=(r, d), device_id_type=MESH))
        copies[-1].start()
    for k in range(1, nr):
        d = lax.rem(r + k, nr)
        copies.append(pltpu.make_async_remote_copy(
            send_ref.at[1, d], got_ref.at[r], s_sem.at[k], r_sem.at[k], device_id=(d, c), device_id_type=MESH))
        copies[-1].start()
    own.wait()
    for cp in copies:
        cp.wait()


def both_exchange(send, term, nr, nc):
    dma = pltpu.SemaphoreType.DMA
    _, order, width = term.shape
    return pl.pallas_call(
        functools.partial(both_exchange_kernel, nr, nc),
        out_shape=(
            jax.ShapeDtypeStruct(send.shape[1:], send.dtype),
            jax.ShapeDtypeStruct((nc, RB_DEV, order, width), term.dtype),
        ),
        in_specs=[VMEM, VMEM],
        out_specs=(VMEM, VMEM),
        scratch_shapes=[dma((nr,)), dma((nr,)), dma((nc,)), dma((nc,)), dma((1,))],
        compiler_params=pltpu.CompilerParams(collective_id=4, has_side_effects=True, vmem_limit_bytes=16 << 20),
    )(send, term)


def gather_sum_kernel(rows_ref, me_ref, got_ref, term_ref, own_ref, acc):
    acc[...] = jnp.zeros_like(acc)

    @pl.loop(0, got_ref.shape[0])
    def _(s):
        row = rows_ref[s]

        @pl.when(row >= 0)
        def _():
            acc[row] = acc[row] + got_ref[s].astype(jnp.float32)

    @pl.loop(0, acc.shape[0])
    def _(b):
        term_ref[b] = acc[b].astype(jnp.bfloat16)

    @pl.loop(0, own_ref.shape[0])
    def _(b):
        own_ref[b] = acc[me_ref[0] * own_ref.shape[0] + b]


def gather_sum(rows, me, got, blocks):
    _, order, width = got.shape
    return pl.pallas_call(
        gather_sum_kernel,
        out_shape=(
            jax.ShapeDtypeStruct((blocks, order, width), jnp.bfloat16),
            jax.ShapeDtypeStruct((RB_DEV, order, width), jnp.float32),
        ),
        in_specs=[SMEM, SMEM, VMEM],
        out_specs=(VMEM, VMEM),
        scratch_shapes=[pltpu.VMEM((blocks, order, width), jnp.float32)],
        compiler_params=pltpu.CompilerParams(vmem_limit_bytes=20 << 20),
    )(rows, me, got)


def greet(nr, nc, r, c):
    barrier = pltpu.get_barrier_semaphore()
    for k in range(1, nr):
        pl.semaphore_signal(barrier, inc=1, device_id=(lax.rem(r + k, nr), c), device_id_type=MESH)
    for k in range(1, nc):
        pl.semaphore_signal(barrier, inc=1, device_id=(r, lax.rem(c + k, nc)), device_id_type=MESH)
    pl.semaphore_wait(barrier, nr - 1 + nc - 1)


def reduce_gram(nr, nc, r, c, gram, landed, cols, full, sems):
    a_s, a_r, b_s, b_r, c_s, c_r = sems
    chunk = gram.shape[0] // nr
    mine = pl.ds(pl.multiple_of(r * chunk, chunk), chunk)
    copies = []
    for k in range(1, nr):
        d = lax.rem(r + k, nr)
        cp = pltpu.make_async_remote_copy(
            gram.at[pl.ds(pl.multiple_of(d * chunk, chunk), chunk), :], landed.at[k], a_s.at[k], a_r.at[k],
            device_id=(d, c), device_id_type=MESH)
        cp.start()
        copies.append(cp)
    total = gram[mine, :]
    for k in range(1, nr):
        copies[k - 1].wait_recv()
        total = total + landed[k]
    cols[c] = total
    across = []
    for k in range(1, nc):
        cp = pltpu.make_async_remote_copy(
            cols.at[c], cols.at[c], b_s.at[k], b_r.at[k], device_id=(r, lax.rem(c + k, nc)), device_id_type=MESH)
        cp.start()
        across.append(cp)
    for cp in across:
        cp.wait_recv()
    total = cols[0]
    for k in range(1, nc):
        total = total + cols[k]
    full[mine, :] = total
    back = []
    for k in range(1, nr):
        cp = pltpu.make_async_remote_copy(
            full.at[mine, :], full.at[mine, :], c_s.at[k], c_r.at[k], device_id=(lax.rem(r + k, nr), c), device_id_type=MESH)
        cp.start()
        back.append(cp)
    for cp in back:
        cp.wait_recv()
    for cp in copies + across + back:
        cp.wait_send()


def gram_scratch(nr, nc, order):
    dma = pltpu.SemaphoreType.DMA
    chunk = order // nr
    return [
        pltpu.VMEM((nr, chunk, order), jnp.float32),
        pltpu.VMEM((nc, chunk, order), jnp.float32),
        pltpu.VMEM((order, order), jnp.float32),
        dma((nr,)), dma((nr,)), dma((nc,)), dma((nc,)), dma((nr,)), dma((nr,)),
    ]


def col_sum_kernel(nr, nc, term_ref, own_ref, arrived0, own0, sketch_ref, out_ref, got, gram, landed, cols, full, *sems):
    r = lax.axis_index("row")
    c = lax.axis_index("col")
    s_sem, r_sem = sems[6], sems[7]
    greet(nr, nc, r, c)
    copies = []
    for k in range(1, nc):
        d = lax.rem(c + k, nc)
        cp = pltpu.make_async_remote_copy(
            term_ref.at[pl.ds(d * RB_DEV, RB_DEV)], got.at[k], s_sem.at[k], r_sem.at[k],
            device_id=(r, d), device_id_type=MESH)
        cp.start()
        copies.append(cp)
    _, order, half = own_ref.shape
    gram[...] = jnp.zeros_like(gram)
    pair = 2 * order

    @pl.loop(0, RB_DEV // 2)
    def _(i):
        pieces = []
        for b in (2 * i, 2 * i + 1):
            total = own0[b]
            for k in range(1, nc):
                total = total + arrived0[k, b].astype(jnp.float32)
            pieces.append(total)
        rows = jnp.concatenate(pieces, axis=0)
        sketch_ref[pl.ds(pl.multiple_of(i * pair, pair), pair), :half] = rows
        gram[:half, :half] += dot_tn(rows, rows)

    for cp in copies:
        cp.wait()

    @pl.loop(0, RB_DEV // 2)
    def _(i):
        pieces = []
        for b in (2 * i, 2 * i + 1):
            total = own_ref[b]
            for k in range(1, nc):
                total = total + got[k, b].astype(jnp.float32)
            pieces.append(total)
        rows = jnp.concatenate(pieces, axis=0)
        part = pl.ds(pl.multiple_of(i * pair, pair), pair)
        sketch_ref[part, half:] = rows
        gram[:, half:] += dot_tn(sketch_ref[part, :], rows)

    gram[half:, :half] = gram[:half, half:].T
    reduce_gram(nr, nc, r, c, gram, landed, cols, full, sems[:6])
    out_ref[...] = full[...]


def col_sum(term, own, arrived0, own0, nr, nc):
    _, order, half = own.shape
    width = HALVES * half
    dma = pltpu.SemaphoreType.DMA
    return pl.pallas_call(
        functools.partial(col_sum_kernel, nr, nc),
        out_shape=(
            jax.ShapeDtypeStruct((RB_DEV * order, width), jnp.float32),
            jax.ShapeDtypeStruct((width, width), jnp.float32),
        ),
        in_specs=[VMEM, VMEM, VMEM, VMEM],
        out_specs=(VMEM, VMEM),
        scratch_shapes=[
            pltpu.VMEM((nc, RB_DEV, order, half), jnp.bfloat16),
            pltpu.VMEM((width, width), jnp.float32),
        ] + gram_scratch(nr, nc, width) + [dma((nc,)), dma((nc,))],
        compiler_params=pltpu.CompilerParams(collective_id=2, has_side_effects=True, vmem_limit_bytes=24 << 20),
    )(term, own, arrived0, own0)


def gram_sum_kernel(nr, nc, gram, out_ref, landed, cols, full, *sems):
    r = lax.axis_index("row")
    c = lax.axis_index("col")
    greet(nr, nc, r, c)
    reduce_gram(nr, nc, r, c, gram, landed, cols, full, sems)
    out_ref[...] = full[...]


def gram_sum(gram, nr, nc):
    return pl.pallas_call(
        functools.partial(gram_sum_kernel, nr, nc),
        out_shape=jax.ShapeDtypeStruct(gram.shape, jnp.float32),
        in_specs=[VMEM],
        out_specs=VMEM,
        scratch_shapes=gram_scratch(nr, nc, gram.shape[0]),
        compiler_params=pltpu.CompilerParams(collective_id=3, has_side_effects=True, vmem_limit_bytes=8 << 20),
    )(gram)


def eliminate(x):
    rows = x.shape[0]
    shape = (8, x.shape[1])
    groups = [x[i:i + 8, :] for i in range(0, rows, 8)]
    sub = lax.broadcasted_iota(jnp.int32, shape, 0)
    for j in range(0, rows, WIDE):
        g, o = divmod(j, 8)
        cols = [[jnp.broadcast_to(groups[i][:, j + l:j + l + 1], shape) for l in range(WIDE)]
                for i in range(g, rows // 8)]
        piv = [[jnp.broadcast_to(cols[0][l][o + k:o + k + 1, :], shape) for l in range(WIDE)] for k in range(WIDE)]
        tops = [jnp.broadcast_to(groups[g][o + k:o + k + 1, :], shape) for k in range(WIDE)]
        recip = []
        for k in range(WIDE):
            recip.append(1.0 / piv[k][k])
            for m in range(k + 1, WIDE):
                q = piv[m][k] * recip[k]
                for l in range(k + 1, WIDE):
                    piv[m][l] = piv[m][l] - q * piv[k][l]
                tops[m] = tops[m] - q * tops[k]
        for i in range(g, rows // 8):
            here = cols[i - g]
            value = groups[i]
            for k in range(WIDE):
                f = here[k] * recip[k]
                for l in range(k + 1, WIDE):
                    here[l] = here[l] - f * piv[k][l]
                value = value - f * tops[k]
            if i == g:
                value = jnp.where(sub >= o + WIDE, value, groups[i])
                for k in range(1, WIDE):
                    value = jnp.where(sub == o + k, tops[k], value)
            groups[i] = value
    return jnp.concatenate(groups, axis=0)


def factor_gram(gram, work, upper, inverse):
    order = gram.shape[0]
    row = lax.broadcasted_iota(jnp.int32, (order, order), 0)
    col = lax.broadcasted_iota(jnp.int32, (order, order), 1)
    work[:, :order] = gram[...]
    work[:, order:] = (row == col).astype(jnp.float32)
    lane = lax.broadcasted_iota(jnp.int32, (PANEL, 2 * PANEL), 1)
    prow = lax.broadcasted_iota(jnp.int32, (PANEL, 2 * PANEL), 0)

    @pl.loop(0, order // PANEL)
    def _(p):
        base = pl.multiple_of(p * PANEL, PANEL)
        tile = work[pl.ds(base, PANEL), pl.ds(pl.multiple_of((p // 2) * 2 * PANEL, 2 * PANEL), 2 * PANEL)]
        tile = jnp.where(p % 2 == 1, pltpu.roll(tile, PANEL, 1), tile)
        x = jnp.where(lane < PANEL, tile, (lane - PANEL == prow).astype(jnp.float32))
        x = eliminate(x)
        diag = jnp.sum(jnp.where(lane == prow, x, 0.0), axis=1, keepdims=True)
        left = pltpu.roll(x, PANEL, 1)[:, :PANEL]
        panel = dot_nn(left, work[pl.ds(base, PANEL), :])
        root = 1.0 / jnp.sqrt(diag)
        pcol = lax.broadcasted_iota(jnp.int32, (PANEL, order), 1)
        pr = lax.broadcasted_iota(jnp.int32, (PANEL, order), 0) + base
        upper[pl.ds(base, PANEL), :] = jnp.where(pcol >= pr, panel[:, :order] * root, 0.0)
        inverse[pl.ds(base, PANEL), :] = jnp.where(pcol <= pr, panel[:, order:] * root, 0.0)

        @pl.when(p < order // PANEL - 1)
        def _():
            half = panel * root
            update = dot_tn(half[:, :order], half)
            below = lax.broadcasted_iota(jnp.int32, (order, 1), 0) >= base + PANEL
            work[...] = jnp.where(below, work[...] - update, work[...])


def first_kernel(gram, sketch, upper, once, second, work, inverse):
    factor_gram(gram, work, upper, inverse)
    second[...] = jnp.zeros_like(second)
    step = 256

    @pl.loop(0, sketch.shape[0] // step)
    def _(i):
        part = pl.ds(pl.multiple_of(i * step, step), step)
        rows = dot_nt(sketch[part, :], inverse[...])
        once[part, :] = rows
        second[...] += dot_tn(rows, rows)


def first_pass(gram, sketch):
    order = gram.shape[0]
    square = jax.ShapeDtypeStruct((order, order), jnp.float32)
    return pl.pallas_call(
        first_kernel,
        out_shape=(square, jax.ShapeDtypeStruct(sketch.shape, jnp.float32), square),
        in_specs=[VMEM, VMEM],
        out_specs=(VMEM, VMEM, VMEM),
        scratch_shapes=[pltpu.VMEM((order, 2 * order), jnp.float32), pltpu.VMEM((order, order), jnp.float32)],
        compiler_params=pltpu.CompilerParams(vmem_limit_bytes=16 << 20),
    )(gram, sketch)


def last_kernel(scale, gram, once, upper_one, basis, factor, work, upper, inverse):
    factor_gram(gram, work, upper, inverse)
    factor[...] = dot_nn(upper[...], upper_one[...]) * (1.0 / scale)
    step = 256

    @pl.loop(0, once.shape[0] // step)
    def _(i):
        part = pl.ds(pl.multiple_of(i * step, step), step)
        basis[part, :] = dot_nt(once[part, :], inverse[...]) * scale


def last_pass(gram, once, upper_one, scale):
    order = gram.shape[0]
    square = pltpu.VMEM((order, order), jnp.float32)
    return pl.pallas_call(
        functools.partial(last_kernel, scale),
        out_shape=(
            jax.ShapeDtypeStruct(once.shape, jnp.float32),
            jax.ShapeDtypeStruct((order, order), jnp.float32),
        ),
        in_specs=[VMEM, VMEM, VMEM],
        out_specs=(VMEM, VMEM),
        scratch_shapes=[pltpu.VMEM((order, 2 * order), jnp.float32), square, square],
        compiler_params=pltpu.CompilerParams(vmem_limit_bytes=16 << 20),
    )(gram, once, upper_one)


def body(nr, nc, a_blocks, omega, route_dest, row_target, col_target):
    targets_here, _, order, _ = a_blocks.shape
    width = omega.shape[1]
    slots = nr * CAP
    destination = route_dest[:, 0]
    positions = jnp.arange(targets_here, dtype=jnp.int32)
    same_owner = destination[:, None] == destination[None, :]
    earlier = positions[None, :] < positions[:, None]
    rank = jnp.sum(jnp.logical_and(same_owner, earlier).astype(jnp.int32), axis=1)
    slot_of = destination * CAP + rank
    slot_ids = jnp.arange(slots, dtype=jnp.int32)
    matches = slot_of[None, :] == slot_ids[:, None]
    send_rows = jnp.sum(jnp.where(matches, row_target[None, :] + 1, 0), axis=1) - 1
    send_rows = jnp.pad(send_rows.reshape(nr, 1, CAP), ((0, 0), (0, 0), (0, 128 - CAP)))
    send_rows = jnp.broadcast_to(send_rows, (nr, 8, 128))
    send = partials(slot_of, col_target.reshape(-1), a_blocks, omega, slots)
    half = width // HALVES
    send = send.reshape(HALVES, nr, CAP, order, half)
    got0, got_rows = row_exchange(send, send_rows, nr)
    me = lax.axis_index("col").astype(jnp.int32).reshape(1)
    rows = got_rows[:, 0, :CAP].reshape(slots)
    term0, own0 = gather_sum(rows, me, got0.reshape(slots, order, half), nc * RB_DEV)
    got1, arrived0 = both_exchange(send, term0, nr, nc)
    term1, own1 = gather_sum(rows, me, got1.reshape(slots, order, half), nc * RB_DEV)
    sketch, gram_one = col_sum(term1, own1, arrived0, own0, nr, nc)
    upper_one, once, gram_part = first_pass(gram_one, sketch)
    gram_two = gram_sum(gram_part, nr, nc)
    scale = float(nr * nc * RB_DEV * order) ** 0.5
    return last_pass(gram_two, once, upper_one, scale)


def solution(mesh):
    nr, nc = mesh.shape["row"], mesh.shape["col"]
    return jax.shard_map(
        functools.partial(body, nr, nc),
        mesh=mesh,
        in_specs=(
            P(("row", "col"), None, None, None),
            P("col", None),
            P(("row", "col"), None),
            P(("row", "col")),
            P(("row", "col"), None),
        ),
        out_specs=(P(("row", "col"), None), P()),
        check_vma=False,
    )
```
